32 devices in a mesh: cube: 4 (over z), row: 2 (over y), col: 4 (over x, core).
Axes of the slice: x: 2, y: 2, z: 4, core: 2. Of those that a mesh axis runs over, the one named last changes fastest.
Arguments:
- diag_block: float32 [4, 512, 512], P('cube', ('row', 'col')), may hold values from -1 to 4, as said below
- panel: float32 [4, 16384, 512], P('cube', 'row', 'col'), may hold values from -2 to 2
- pattern: int32 [4, 128, 4], P('cube', 'row', 'col'), may hold values 0 or 1
- contribution: float32 [4, 16384, 512], P('cube', 'row', 'col'), may hold values from -6 to 6
- route: int32 [4, 128, 1], P('cube', 'row'), may hold values from 0 to 3; in each aligned block of 64 rows (0 to 63, 64 to 127, ..., all dimensions but the last counted through in order) at most 32 rows name the same one
- slot: int32 [4, 128], P('cube', 'row'), may hold values from 0 to 31
Outputs:
- diag_factor: float32 [4, 512, 512], P('cube', ('row', 'col'))
- panel_factor: float32 [4, 16384, 512], P('cube', 'row', 'col')
- assembled: float32 [4, 8192, 512], P('cube', 'row', 'col')
The draws below stay inside these ranges and needn't reach their ends.
Inputs may be any that keep to these rules, and one draw needn't show every extreme that they name: `diag_block`: each 512 x 512 block is symmetric with positive diagonal larger than the sum of magnitudes of the rest of its row. `route`: within the 64 rows of one device, no value names more than 32 blocks.
All inputs are finite; a program needn't handle non-finite values. No bound on the sum of `pattern` on one device may be relied on, other than what follows from the above.
Results may differ from the reference program's by a relative error of at most 0.0001.
Values sent between devices are 32-bit elements; how exact they have to be, the bound alone decides.
A program may use at most 128 MiB of HBM per device.

```python
import math
import jax
import jax.numpy as jnp
import numpy as np
from jax import lax

PB = 512
M = 16384
BS = 128
CW = 512
FRONTS = 4
MB = 128
BLK_DEV = 64
CAP = 32
PBLK = 32
N_CUBE = 4
N_ROW = 2


def draw_diag_block(key, part):
    first = jax.random.fold_in(jax.random.fold_in(key, 11), 0)
    second = jax.random.fold_in(jax.random.fold_in(key, 11), 1)
    fourth = jax.random.fold_in(jax.random.fold_in(key, 11), 3)
    ident = jnp.eye(PB, dtype=jnp.float32)[None]
    index_rows = jnp.arange(PB, dtype=jnp.int32)[:, None]
    index_cols = jnp.arange(PB, dtype=jnp.int32)[None, :]
    distance = jnp.abs(index_rows - index_cols)
    heights = jax.random.uniform(second, (N_CUBE, PB), jnp.float32, 2.5, 3.5)
    coupling = jax.random.uniform(first, (N_CUBE, PB, PB), jnp.float32, 0.5, 1.0)
    coupling = 0.5 * (coupling + jnp.swapaxes(coupling, 1, 2))
    banded = ((distance >= 1) & (distance <= 3)).astype(jnp.float32)[None]
    scatter = jax.random.uniform(fourth, (N_CUBE, PB, PB), jnp.float32, -1.0, 1.0)
    scatter = 0.5 * (scatter + jnp.swapaxes(scatter, 1, 2))
    offdiag = coupling * banded * 0.36 + scatter * (0.3 / PB)
    return offdiag * (1.0 - ident) + ident * heights[:, :, None]


def set_ends(result, own_key, low, largest):
    spot = [jax.random.randint(jax.random.fold_in(own_key, axis), (), 0, length) for axis, length in enumerate(result.shape)]
    main_axis = result.shape.index(max(result.shape))
    neighbour = spot[:main_axis] + [(spot[main_axis] + 1) % result.shape[main_axis]] + spot[main_axis + 1:]
    return result.at[tuple(spot)].set(low).at[tuple(neighbour)].set(largest)


def level_of(key, extent, pieces, smallest, high):
    factor_of = 1.0
    for dim, blocks in pieces:
        steps = jax.random.uniform(jax.random.fold_in(jax.random.fold_in(key, 6), dim), (blocks,), jnp.float32, smallest / len(pieces), high / len(pieces))
        factor_of = factor_of * jnp.repeat(jnp.exp(steps), extent[dim] // blocks).reshape((-1,) + (1,) * (len(extent) - 1 - dim))
    return factor_of


def deal_out(own_key, own, number, rows, number_of, top, limit, slope):
    order = jax.random.permutation(own_key, number_of)
    packed, common = shares(number_of, rows * top, limit, slope, True), shares(number_of, rows * top, limit, slope, False)
    places = jnp.arange(number_of)

    def named(tallies, rotation):
        used = int((tallies > 0).sum())
        fixed = max(1, used // 4)
        shifted = fixed + (places - fixed + rotation * (used - fixed)) % max(1, number_of - fixed)
        return jnp.zeros((number_of,), jnp.int32).at[order[jnp.where(places < fixed, places, shifted)]].set(jnp.asarray(tallies, jnp.int32))

    tallies = jnp.where(number % 4 == 0, named(packed, number // 4), named(common, number - number // 4 - 1))
    mixed = jax.random.permutation(jax.random.fold_in(own, 3), number_of)
    donor, sink = mixed[0:number_of // 2 * 2:2], mixed[1:number_of // 2 * 2:2]
    margin = jnp.minimum(tallies[donor] - 1, limit - tallies[sink]) // 2
    margin = jnp.where((donor == order[0]) | (sink == order[0]) | (tallies[sink] == 0), 0, jnp.maximum(margin, 0))
    shifted = jax.random.randint(jax.random.fold_in(own, 4), (number_of // 2,), 0, 1 << 20) % (margin + 1)
    tallies = tallies.at[donor].add(-shifted).at[sink].add(shifted)
    labels = jnp.searchsorted(jnp.cumsum(tallies), jnp.arange(rows * top), side="right").astype(jnp.int32)
    listing = labels.reshape(top, rows).T
    listing = listing[jax.random.permutation(jax.random.fold_in(own, 1), rows)]
    rotation = jax.random.randint(jax.random.fold_in(own, 2), (rows, 1), 0, top)
    return jnp.take_along_axis(listing, (jnp.arange(top)[None, :] + rotation) % top, axis=1)


def shares(amount, total, bound, lean, full):
    portions = [(1 << 20) // math.isqrt(grade ** lean) + 1 for grade in range(1, amount + 1)]
    largest = bound if full else min(bound, max(-(-total // amount), total * portions[0] // sum(portions)))
    least = 1 if total - largest >= amount - 1 else 0
    given, rest = [largest] + [least] * (amount - 1), total - largest - least * (amount - 1)
    while rest > 0:
        candidates = [i for i in range(1, amount) if given[i] < largest] or [i for i in range(1, amount) if given[i] < bound]
        whole, budget = sum([portions[i] for i in candidates]), rest
        for i in candidates:
            extra = min(bound - given[i], max(1, budget * portions[i] // whole), rest)
            given[i] = given[i] + extra
            rest = rest - extra
    return np.array(given)


def noise(stream_key, shape, spread, bound, pieces=(), kind=jnp.bfloat16):
    level = level_of(stream_key, shape, pieces, -0.22, 0.18) if pieces else 1.0
    values = jax.random.normal(stream_key, shape, jnp.float32) * spread * level
    return jnp.minimum(jnp.maximum(values, -bound), bound).astype(kind)


def setup_inputs(seed: int = 0) -> dict:
    splits = jax.random.split(jax.random.key(seed), 7)
    diag_block = draw_diag_block(jax.random.fold_in(splits[6], 71), 0)
    panel = noise(splits[1], (FRONTS, M, PB), (max(1, PB // 64)) ** -0.5, 2.0, ((0, 4), (1, 2), (2, 4)), jnp.float32)
    pattern = set_ends((jax.random.randint(splits[2], (FRONTS, MB, PB // BS), 0, 4) < 3).astype(jnp.int32), jax.random.fold_in(splits[2], 1), 0, 1)
    contribution = noise(splits[3], (FRONTS, M, CW), 1.0, 6.0, ((0, 4), (1, 2), (2, 4)), jnp.float32)
    route_keys = jax.random.split(jax.random.fold_in(splits[4], 1), FRONTS * MB // BLK_DEV)
    route_turns = jax.random.permutation(jax.random.fold_in(splits[4], 3), FRONTS * MB // BLK_DEV)
    route = jax.vmap(lambda own, number: deal_out(jax.random.fold_in(splits[4], 2), own, number, BLK_DEV, 2 * N_ROW, 1, CAP, 0))(route_keys, route_turns).reshape((FRONTS, MB, 1))
    slot = set_ends(jax.random.randint(splits[5], (FRONTS, MB), 0, PBLK), jax.random.fold_in(splits[5], 1), 0, PBLK - 1).astype(jnp.int32)
    return {"diag_block": diag_block, "panel": panel, "pattern": pattern, "contribution": contribution, "route": route, "slot": slot}


def reference(diag_block, panel, pattern, contribution, route, slot):
    highest = lax.Precision.HIGHEST
    factors = []
    panels = []
    updates = []
    for front in range(N_CUBE):
        lower = jnp.linalg.cholesky(diag_block[front])
        inverse = jax.scipy.linalg.solve_triangular(lower, jnp.eye(PB, dtype=jnp.float32), lower=True)
        tile_mask = jnp.repeat(jnp.repeat(pattern[front], BS, axis=0), BS, axis=1).astype(jnp.float32)
        masked = panel[front] * tile_mask
        factor_rows = jnp.dot(masked, inverse.T, precision=highest)
        update = contribution[front] - jnp.dot(factor_rows, factor_rows[:CW].T, precision=highest)
        factors.append(lower)
        panels.append(factor_rows)
        updates.append(update)
    halves = []
    for parent_index in range(N_CUBE // 2):
        total = jnp.zeros((MB, BS * CW), jnp.float32)
        for child in (2 * parent_index, 2 * parent_index + 1):
            blocks = updates[child].reshape(MB, BS * CW)
            target = (route[child, :, 0] * PBLK + slot[child]).astype(jnp.int32)
            total = total.at[target].add(blocks)
        total = total.reshape(2, M // 2, CW)
        halves.append(total[0])
        halves.append(total[1])
    return (jnp.stack(factors), jnp.stack(panels), jnp.stack(halves))
```

```python
import functools

import jax
import jax.numpy as jnp
from jax import lax
from jax.experimental import pallas as pl
from jax.experimental.pallas import tpu as pltpu
from jax.sharding import PartitionSpec as P

BS = 128
HIGHEST = lax.Precision.HIGHEST
NT = (((1,), (1,)), ((), ()))
ANY = pl.BlockSpec(memory_space=pl.ANY)
VMEM = pl.BlockSpec(memory_space=pltpu.VMEM)
MESH = pl.DeviceIdType.MESH


def remote(src, dst, send, recv, device):
    return pltpu.make_async_remote_copy(
        src_ref=src, dst_ref=dst, send_sem=send, recv_sem=recv,
        device_id=device, device_id_type=MESH,
    )


def factor_block(s_ref, x_ref):
    n = BS
    sub = lax.broadcasted_iota(jnp.int32, (n, n), 0)
    lane = lax.broadcasted_iota(jnp.int32, (n, n), 1)
    x_ref[...] = (sub == lane).astype(jnp.float32)
    step = 32
    for lo in range(0, n, step):
        rows = n - lo
        lane_r = lax.broadcasted_iota(jnp.int32, (rows, n), 1)
        sub_c = lax.broadcasted_iota(jnp.int32, (rows, 1), 0) + lo
        lane_1 = lax.broadcasted_iota(jnp.int32, (1, n), 1)

        def body(j, carry):
            s = s_ref[pl.ds(lo, rows), :]
            x = x_ref[pl.ds(lo, rows), :]
            row_s = s_ref[pl.ds(j, 1), :]
            row_x = x_ref[pl.ds(j, 1), :]
            col = jnp.sum(jnp.where(lane_r == j, s, 0.0), axis=1, keepdims=True)
            pivot = jnp.sum(jnp.where(lane_1 == j, row_s, 0.0), axis=1, keepdims=True)
            scale = 1.0 / pivot
            col = jnp.where(sub_c > j, col, 0.0)
            s_ref[pl.ds(lo, rows), :] = s - col * (row_s * scale)
            x_ref[pl.ds(lo, rows), :] = x - col * (row_x * scale)
            return carry

        lax.fori_loop(lo, lo + step, body, 0)


def cholesky_inverse(a_ref, inv_ref, s_ref, x_ref, between):
    width = a_ref.shape[0]
    sub = lax.broadcasted_iota(jnp.int32, (BS, BS), 0)
    lane = lax.broadcasted_iota(jnp.int32, (BS, BS), 1)
    inv_ref[...] = jnp.zeros_like(inv_ref)
    for p in range(width // BS):
        o, e = p * BS, (p + 1) * BS
        s_ref[...] = a_ref[o:e, o:e]
        factor_block(s_ref, x_ref)
        s = s_ref[...]
        d = jnp.sum(jnp.where(lane == sub, s, 0.0), axis=1, keepdims=True)
        rs = 1.0 / jnp.sqrt(d)
        low = jnp.transpose(jnp.where(lane >= sub, s, 0.0) * rs)
        x = x_ref[...] * rs
        a_ref[o:e, o:e] = low
        inv_ref[o:e, o:e] = x
        if e < width:
            below = lax.dot_general(a_ref[e:, o:e], x, NT, precision=HIGHEST)
            a_ref[e:, o:e] = below
            a_ref[e:, e:] = a_ref[e:, e:] - lax.dot_general(below, below, NT, precision=HIGHEST)
            a_ref[o:e, e:] = jnp.zeros((BS, width - e), jnp.float32)
        if p > 0:
            part = jnp.dot(a_ref[o:e, :o], inv_ref[:o, :o], precision=HIGHEST)
            inv_ref[o:e, :o] = -jnp.dot(x, part, precision=HIGHEST)
        between(p)


def gather_kernel(chunks, diag_ref, panel_ref, g0_ref, g1_ref, g2_ref, l_ref, v_ref,
                  a_ref, inv_ref, s_ref, x_ref, h_ref, hc_ref, w_ref,
                  dsend, drecv, xsend, xrecv, fsend, frecv, psend, precv, hsend, hrecv, lsem):
    r, c = lax.axis_index("row"), lax.axis_index("col")
    y = 1 - r
    c1 = c + 1 - 2 * (c % 2)
    c2 = (c + 2) % 4
    c3 = (c1 + 2) % 4
    order = (c, c1, c2, c3)
    ndiag = diag_ref.shape[0]
    rows = panel_ref.shape[0] // chunks

    barrier = pltpu.get_barrier_semaphore()
    for rr in (r, y):
        for cc in order:
            if not (rr is r and cc is c):
                pl.semaphore_signal(barrier, inc=1, device_id={"row": rr, "col": cc}, device_id_type=MESH)
    pl.semaphore_wait(barrier, 7)

    def spot(rr, cc):
        return a_ref.at[pl.ds(pl.multiple_of((rr * 4 + cc) * ndiag, ndiag), ndiag)]

    def diag_copy(k, src, rr, cc, device):
        return remote(src, spot(rr, cc), dsend.at[k], drecv.at[k], device)

    first = diag_copy(0, diag_ref, r, c, {"row": r, "col": c2})
    first.start()
    across = [
        remote(panel_ref.at[pl.ds(i * rows, rows)], g1_ref.at[pl.ds(i * rows, rows)],
               xsend.at[i], xrecv.at[i], {"row": r, "col": c2})
        for i in range(chunks)
    ]
    onward = [
        remote(g1_ref.at[pl.ds(i * rows, rows)], g2_ref.at[pl.ds(i * rows, rows)],
               fsend.at[i], frecv.at[i], {"row": r, "col": c1})
        for i in range(chunks)
    ]
    own = remote(panel_ref, g0_ref, psend, precv, {"row": r, "col": c1})
    for copy in across:
        copy.start()
    second = [diag_copy(1, diag_ref, r, c, {"row": y, "col": c})]
    second[0].start()
    a_ref[pl.ds(pl.multiple_of((r * 4 + c) * ndiag, ndiag), ndiag), :] = diag_ref[...]
    first.wait_recv()
    second.append(diag_copy(2, spot(r, c2), r, c2, {"row": y, "col": c}))
    second[1].start()
    third = [
        diag_copy(3, diag_ref, r, c, {"row": r, "col": c1}),
        diag_copy(4, spot(r, c2), r, c2, {"row": r, "col": c1}),
    ]
    for copy in third:
        copy.start()
    for k, copy in enumerate(second):
        copy.wait_recv()
    third.append(diag_copy(5, spot(y, c), y, c, {"row": r, "col": c1}))
    third.append(diag_copy(6, spot(y, c2), y, c2, {"row": r, "col": c1}))
    for copy in third[2:]:
        copy.start()
    for copy in third:
        copy.wait_recv()
    for copy in [first] + second + third:
        copy.wait_send()
    own.start()

    def between(p):
        across[p].wait_recv()
        onward[p].start()

    cholesky_inverse(a_ref, inv_ref, s_ref, x_ref, between)
    l_ref[...] = a_ref[pl.ds(pl.multiple_of((r * 4 + c) * ndiag, ndiag), ndiag), :]

    own.wait_recv()
    onward[0].wait_recv()
    head = remote(h_ref, h_ref, hsend, hrecv, {"row": y, "col": c})

    @pl.when(r == 0)
    def _():
        window = pl.ds(pl.multiple_of(c * BS, BS), BS)
        loads = [
            pltpu.make_async_copy(src.at[window], h_ref.at[j], lsem.at[j])
            for j, src in enumerate((panel_ref, g0_ref, g1_ref, g2_ref))
        ]
        for copy in loads:
            copy.start()
        for copy in loads:
            copy.wait()
        head.start()
        head.wait_send()

    @pl.when(r == 1)
    def _():
        head.wait_recv()

    for i in range(4, chunks):
        across[i].wait_recv()
        onward[i].start()
    for j, k in enumerate(order):
        hc_ref[:, pl.ds(pl.multiple_of(k * BS, BS), BS)] = h_ref[j]
    factor_head = lax.dot_general(hc_ref[...], inv_ref[...], NT, precision=HIGHEST)
    w_ref[pl.ds(BS, BS), :] = jnp.dot(factor_head, inv_ref[...], precision=HIGHEST)
    w_ref[pl.ds(0, BS), :] = inv_ref[pl.ds(pl.multiple_of(c * BS, BS), BS), :]
    for j, k in enumerate(order):
        v_ref[j] = w_ref[:, pl.ds(pl.multiple_of(k * BS, BS), BS)]
    for i in range(1, chunks):
        onward[i].wait_recv()
    for i in range(chunks):
        across[i].wait_send()
        onward[i].wait_send()
    own.wait_send()


def gather_and_factor(diag, masked):
    chunks = 8
    rows, share = masked.shape
    ndiag, width = diag.shape
    piece = jax.ShapeDtypeStruct((rows, share), jnp.float32)
    return pl.pallas_call(
        functools.partial(gather_kernel, chunks),
        out_shape=(
            piece, piece, piece,
            jax.ShapeDtypeStruct((ndiag, width), jnp.float32),
            jax.ShapeDtypeStruct((4, 2 * BS, BS), jnp.float32),
        ),
        in_specs=[VMEM, ANY],
        out_specs=(ANY, ANY, ANY, VMEM, VMEM),
        scratch_shapes=[
            pltpu.VMEM((width, width), jnp.float32),
            pltpu.VMEM((width, width), jnp.float32),
            pltpu.VMEM((BS, BS), jnp.float32),
            pltpu.VMEM((BS, BS), jnp.float32),
            pltpu.VMEM((4, BS, BS), jnp.float32),
            pltpu.VMEM((BS, width), jnp.float32),
            pltpu.VMEM((2 * BS, width), jnp.float32),
            pltpu.SemaphoreType.DMA((7,)),
            pltpu.SemaphoreType.DMA((7,)),
            pltpu.SemaphoreType.DMA((chunks,)),
            pltpu.SemaphoreType.DMA((chunks,)),
            pltpu.SemaphoreType.DMA((chunks,)),
            pltpu.SemaphoreType.DMA((chunks,)),
            pltpu.SemaphoreType.DMA,
            pltpu.SemaphoreType.DMA,
            pltpu.SemaphoreType.DMA,
            pltpu.SemaphoreType.DMA,
            pltpu.SemaphoreType.DMA((4,)),
        ],
        compiler_params=pltpu.CompilerParams(collective_id=0, has_side_effects=True),
        name="gather_factor",
    )(diag, masked)


def split(value):
    high = value.astype(jnp.bfloat16)
    return high, (value - high.astype(jnp.float32)).astype(jnp.bfloat16)


def update_kernel(tile, goal_ref, own_ref, g0_ref, g1_ref, g2_ref, contribution_ref, v_ref,
                  f_ref, t_ref, vh_ref, vl_ref):
    step = pl.program_id(0)

    @pl.when(step == 0)
    def _():
        t_ref[...] = jnp.zeros_like(t_ref)
        for j in range(4):
            high, low = split(v_ref[j])
            vh_ref[:, j * BS:(j + 1) * BS] = high
            vl_ref[:, j * BS:(j + 1) * BS] = low

    full = jnp.concatenate([own_ref[...], g0_ref[...], g1_ref[...], g2_ref[...]], axis=1)
    high, low = split(full)
    dot = functools.partial(lax.dot_general, dimension_numbers=NT, preferred_element_type=jnp.float32)
    out = dot(high, vh_ref[...]) + (dot(high, vl_ref[...]) + dot(low, vh_ref[...]))
    f_ref[...] = out[:, :BS]
    update = contribution_ref[...] - out[:, BS:]
    for b in range(tile // BS):
        goal = goal_ref[step * (tile // BS) + b]
        t_ref[goal] = t_ref[goal] + update[b * BS:(b + 1) * BS]


def update_and_pack(goal, masked, pieces, contribution, v, slots):
    tile = 512
    rows, share = masked.shape
    block = pl.BlockSpec((tile, share), lambda i, g: (i, 0))
    return pl.pallas_call(
        functools.partial(update_kernel, tile),
        out_shape=(
            jax.ShapeDtypeStruct((rows, share), jnp.float32),
            jax.ShapeDtypeStruct((slots, BS, share), jnp.float32),
        ),
        grid_spec=pltpu.PrefetchScalarGridSpec(
            num_scalar_prefetch=1,
            grid=(rows // tile,),
            in_specs=[block] * 5 + [pl.BlockSpec(v.shape, lambda i, g: (0, 0, 0))],
            out_specs=(block, pl.BlockSpec((slots, BS, share), lambda i, g: (0, 0, 0))),
            scratch_shapes=[pltpu.VMEM((2 * BS, 4 * BS), jnp.bfloat16)] * 2,
        ),
        compiler_params=pltpu.CompilerParams(dimension_semantics=("arbitrary",)),
        name="update_pack",
    )(goal, masked, *pieces, contribution, v)


def route_kernel(t_ref, out_ref, ra, rb, ra2, rb2, asend, arecv, bsend, brecv,
                 a2send, a2recv, b2send, b2recv):
    z, r = lax.axis_index("cube"), lax.axis_index("row")
    m, y = z % 2, 1 - r
    dev_y = {"row": y}
    dev_z = {"cube": z + 1 - 2 * m}
    barrier = pltpu.get_barrier_semaphore()
    for device in (dev_y, dev_z):
        pl.semaphore_signal(barrier, inc=1, device_id=device, device_id_type=MESH)
    pl.semaphore_wait(barrier, 2)
    half = t_ref.shape[1] // 2
    n = 8
    parts = half // n
    over_a, over_b = {}, {}
    for rel in range(2):
        for k in range(parts):
            h = (1 - m) if rel == 0 else m
            over_a[rel, k] = remote(
                t_ref.at[h * 2 + y, pl.ds(k * n, n)], ra.at[rel, pl.ds(k * n, n)],
                asend.at[rel, k], arecv.at[rel, k], dev_y)
            rr = y if rel == 0 else r
            over_b[rel, k] = remote(
                t_ref.at[(1 - m) * 2 + rr, pl.ds(half + k * n, n)], rb.at[rel, pl.ds(k * n, n)],
                bsend.at[rel, k], brecv.at[rel, k], dev_z)
            over_a[rel, k].start()
            over_b[rel, k].start()
    last = {}
    for k in range(parts):
        part = pl.ds(k * n, n)
        other = pl.ds(half + k * n, n)
        over_a[0, k].wait_recv()
        ra[0, part] = ra[0, part] + t_ref[(1 - m) * 2 + r, part]
        over_b[0, k].wait_recv()
        rb[0, part] = rb[0, part] + t_ref[m * 2 + y, other]
        last[0, k] = remote(ra.at[0, part], ra2.at[part], a2send.at[k], a2recv.at[k], dev_z)
        last[1, k] = remote(rb.at[0, part], rb2.at[part], b2send.at[k], b2recv.at[k], dev_y)
        last[0, k].start()
        last[1, k].start()
    for k in range(parts):
        part = pl.ds(k * n, n)
        other = pl.ds(half + k * n, n)
        over_a[1, k].wait_recv()
        out_ref[part] = t_ref[m * 2 + r, part] + ra[1, part]
        over_b[1, k].wait_recv()
        out_ref[other] = t_ref[m * 2 + r, other] + rb[1, part]
    for k in range(parts):
        part = pl.ds(k * n, n)
        other = pl.ds(half + k * n, n)
        last[0, k].wait_recv()
        out_ref[part] = out_ref[part] + ra2[part]
        last[1, k].wait_recv()
        out_ref[other] = out_ref[other] + rb2[part]
    for copy in list(over_a.values()) + list(over_b.values()) + list(last.values()):
        copy.wait_send()


def route_blocks(packed):
    _, slots, rows, share = packed.shape
    half = slots // 2
    parts = half // 8
    return pl.pallas_call(
        route_kernel,
        out_shape=jax.ShapeDtypeStruct((slots, rows, share), jnp.float32),
        in_specs=[VMEM],
        out_specs=VMEM,
        scratch_shapes=[
            pltpu.VMEM((2, half, rows, share), jnp.float32),
            pltpu.VMEM((2, half, rows, share), jnp.float32),
            pltpu.VMEM((half, rows, share), jnp.float32),
            pltpu.VMEM((half, rows, share), jnp.float32),
            pltpu.SemaphoreType.DMA((2, parts)),
            pltpu.SemaphoreType.DMA((2, parts)),
            pltpu.SemaphoreType.DMA((2, parts)),
            pltpu.SemaphoreType.DMA((2, parts)),
            pltpu.SemaphoreType.DMA((parts,)),
            pltpu.SemaphoreType.DMA((parts,)),
            pltpu.SemaphoreType.DMA((parts,)),
            pltpu.SemaphoreType.DMA((parts,)),
        ],
        compiler_params=pltpu.CompilerParams(collective_id=1, has_side_effects=True),
        name="route_blocks",
    )(packed)


def mask_panel(panel, pattern):
    tile_mask = jnp.repeat(jnp.repeat(pattern[0], BS, axis=0), BS, axis=1).astype(jnp.float32)
    return panel[0] * tile_mask


def on_small(diag_block, panel, pattern, contribution, route, slot):
    masked = mask_panel(panel, pattern)
    blk = masked.shape[0] // BS
    pblk = blk // 2
    nrow = lax.axis_size("row")
    goal = (route[0, :, 0] * pblk + slot[0]).astype(jnp.int32)
    g0, g1, g2, lower, v = gather_and_factor(diag_block[0], masked)
    factor, packed = update_and_pack(goal, masked, (g0, g1, g2), contribution[0], v, 2 * nrow * pblk)
    share = masked.shape[1]
    assembled = route_blocks(packed.reshape(2 * nrow, pblk, BS, share))
    return (lower[None], factor[None], assembled.reshape(1, pblk * BS, share))


def from_root(value, axis, root):
    mine = lax.axis_index(axis) == root
    return lax.psum(jnp.where(mine, value, jnp.zeros_like(value)), axis)


def partner(value, axis, apart):
    mask = 2**apart
    pairs = [(source, source ^ mask) for source in range(lax.axis_size(axis))]
    return lax.ppermute(value, axis, pairs)


def on_large(diag_block, panel, pattern, contribution, route, slot):
    highest = lax.Precision.HIGHEST
    contract = (((1,), (1,)), ((), ()))
    whole = lax.all_gather(diag_block, ("row", "col"), axis=1, tiled=True)[0]
    width = whole.shape[0]
    lower = jnp.linalg.cholesky(whole)
    inverse = jax.scipy.linalg.solve_triangular(
        lower, jnp.eye(width, dtype=jnp.float32), lower=True
    )
    ncol = lax.axis_size("col")
    nrow = lax.axis_size("row")
    col_index = lax.axis_index("col")
    tile_mask = jnp.repeat(jnp.repeat(pattern[0], BS, axis=0), BS, axis=1).astype(jnp.float32)
    masked = panel[0] * tile_mask
    rows_dev = masked.shape[0]
    full_rows = lax.all_gather(masked, "col", axis=1, tiled=True)
    factor_rows = lax.dot_general(full_rows, inverse, contract, precision=highest)
    share = width // ncol
    own_cols = lax.dynamic_slice_in_dim(factor_rows, col_index * share, share, 1)
    cw_dev = contribution.shape[2]
    head_piece = lax.dynamic_slice_in_dim(factor_rows, col_index * cw_dev, cw_dev, 0)
    head_rows = from_root(head_piece, "row", 0)
    update = contribution[0] - lax.dot_general(factor_rows, head_rows, contract, precision=highest)
    blk = rows_dev // BS
    cap = max(2, blk // nrow)
    pblk = blk // 2
    blocks = update.reshape(blk, BS * cw_dev)
    target = route[0, :, 0]
    place = slot[0]
    order_ids = jnp.arange(blk, dtype=jnp.int32)
    earlier = (target[None, :] == target[:, None]) & (order_ids[None, :] < order_ids[:, None])
    rank = jnp.sum(earlier.astype(jnp.int32), axis=1)
    half = target // nrow
    target_row = target % nrow
    position = target_row * (2 * cap) + half * cap + rank
    slots_all = jnp.arange(nrow * 2 * cap, dtype=jnp.int32)
    onehot = (position[None, :] == slots_all[:, None]).astype(jnp.float32)
    packed = jnp.dot(onehot, blocks, precision=highest).reshape(nrow, 2, cap, BS * cw_dev)
    labels = jnp.dot(onehot, (place + 1).astype(jnp.float32), precision=highest).reshape(
        nrow, 2, cap
    )
    mine = lax.axis_index("cube") % 2
    got, got_labels = (
        lax.all_to_all(packed, "row", split_axis=0, concat_axis=0, tiled=True),
        lax.all_to_all(labels, "row", split_axis=0, concat_axis=0, tiled=True),
    )
    keep = lax.dynamic_index_in_dim(got, mine, 1, keepdims=False)
    keep_labels = lax.dynamic_index_in_dim(got_labels, mine, 1, keepdims=False)
    other = lax.dynamic_index_in_dim(got, 1 - mine, 1, keepdims=False)
    other_labels = lax.dynamic_index_in_dim(got_labels, 1 - mine, 1, keepdims=False)
    back, back_labels = partner((other, other_labels), "cube", 0)
    incoming = jnp.concatenate([keep, back], axis=0).reshape(-1, BS * cw_dev)
    tags = jnp.concatenate([keep_labels, back_labels], axis=0).reshape(-1)
    wanted = jnp.arange(1, pblk + 1, dtype=jnp.float32)
    select = (tags[None, :] == wanted[:, None]).astype(jnp.float32)
    assembled = jnp.dot(select, incoming, precision=highest).reshape(pblk * BS, cw_dev)
    rows_here = diag_block.shape[1]
    diag_rows = lax.dynamic_slice_in_dim(
        lower, lax.axis_index(("row", "col")) * rows_here, rows_here, 0
    )
    return (diag_rows[None], own_cols[None], assembled[None])


def solution(mesh):
    small = mesh.shape["row"] == 2 and mesh.shape["col"] == 4
    return jax.shard_map(
        on_small if small else on_large,
        mesh=mesh,
        in_specs=(
            P("cube", ("row", "col"), None),
            P("cube", "row", "col"),
            P("cube", "row", "col"),
            P("cube", "row", "col"),
            P("cube", "row", None),
            P("cube", "row"),
        ),
        out_specs=(
            P("cube", ("row", "col"), None),
            P("cube", "row", "col"),
            P("cube", "row", "col"),
        ),
        check_vma=False,
    )
```

```python
import functools

import jax
import jax.numpy as jnp
from jax import lax
from jax.experimental import pallas as pl
from jax.experimental.pallas import tpu as pltpu
from jax.sharding import PartitionSpec as P

BS = 128
HIGHEST = lax.Precision.HIGHEST
NT = (((1,), (1,)), ((), ()))
ANY = pl.BlockSpec(memory_space=pl.ANY)
VMEM = pl.BlockSpec(memory_space=pltpu.VMEM)
MESH = pl.DeviceIdType.MESH


def remote(src, dst, send, recv, device):
    return pltpu.make_async_remote_copy(
        src_ref=src, dst_ref=dst, send_sem=send, recv_sem=recv,
        device_id=device, device_id_type=MESH,
    )


def factor_block(s_ref, x_ref):
    n = BS
    sub = lax.broadcasted_iota(jnp.int32, (n, n), 0)
    lane = lax.broadcasted_iota(jnp.int32, (n, n), 1)
    x_ref[...] = (sub == lane).astype(jnp.float32)
    step = 32
    for lo in range(0, n, step):
        rows = n - lo
        lane_r = lax.broadcasted_iota(jnp.int32, (rows, n), 1)
        sub_c = lax.broadcasted_iota(jnp.int32, (rows, 1), 0) + lo
        lane_1 = lax.broadcasted_iota(jnp.int32, (1, n), 1)

        def body(j, carry):
            s = s_ref[pl.ds(lo, rows), :]
            x = x_ref[pl.ds(lo, rows), :]
            row_s = s_ref[pl.ds(j, 1), :]
            row_x = x_ref[pl.ds(j, 1), :]
            col = jnp.sum(jnp.where(lane_r == j, s, 0.0), axis=1, keepdims=True)
            pivot = jnp.sum(jnp.where(lane_1 == j, row_s, 0.0), axis=1, keepdims=True)
            scale = 1.0 / pivot
            col = jnp.where(sub_c > j, col, 0.0)
            s_ref[pl.ds(lo, rows), :] = s - col * (row_s * scale)
            x_ref[pl.ds(lo, rows), :] = x - col * (row_x * scale)
            return carry

        lax.fori_loop(lo, lo + step, body, 0)


def cholesky_inverse(a_ref, inv_ref, s_ref, x_ref, between):
    width = a_ref.shape[0]
    sub = lax.broadcasted_iota(jnp.int32, (BS, BS), 0)
    lane = lax.broadcasted_iota(jnp.int32, (BS, BS), 1)
    inv_ref[...] = jnp.zeros_like(inv_ref)
    for p in range(width // BS):
        o, e = p * BS, (p + 1) * BS
        s_ref[...] = a_ref[o:e, o:e]
        factor_block(s_ref, x_ref)
        s = s_ref[...]
        d = jnp.sum(jnp.where(lane == sub, s, 0.0), axis=1, keepdims=True)
        rs = 1.0 / jnp.sqrt(d)
        low = jnp.transpose(jnp.where(lane >= sub, s, 0.0) * rs)
        x = x_ref[...] * rs
        a_ref[o:e, o:e] = low
        inv_ref[o:e, o:e] = x
        if e < width:
            below = lax.dot_general(a_ref[e:, o:e], x, NT, precision=HIGHEST)
            a_ref[e:, o:e] = below
            a_ref[e:, e:] = a_ref[e:, e:] - lax.dot_general(below, below, NT, precision=HIGHEST)
            a_ref[o:e, e:] = jnp.zeros((BS, width - e), jnp.float32)
        if p > 0:
            part = jnp.dot(a_ref[o:e, :o], inv_ref[:o, :o], precision=HIGHEST)
            inv_ref[o:e, :o] = -jnp.dot(x, part, precision=HIGHEST)
        between(p)


def gather_kernel(chunks, diag_ref, mask_ref, panel_ref, contribution_ref, f_ref, u_ref, l_ref,
                  own, g0, g1, g2, contrib, a_ref, inv_ref, s_ref, x_ref, h_ref, hc_ref, w_ref,
                  vh_ref, vl_ref, masks, head_masks, fs, us,
                  dsend, drecv, xsend, xrecv, fsend, frecv, psend, precv, hsend, hrecv,
                  msend, mrecv, lsem, isem, osem):
    r, c = lax.axis_index("row"), lax.axis_index("col")
    y = 1 - r
    c1 = c + 1 - 2 * (c % 2)
    c2 = (c + 2) % 4
    c3 = (c1 + 2) % 4
    order = (c, c1, c2, c3)
    pieces = (own, g0, g1, g2)
    ndiag = diag_ref.shape[0]
    rows = panel_ref.shape[0] // chunks
    to_x, to_core, to_row = {"col": c2}, {"col": c1}, {"row": y}

    load_own = pltpu.make_async_copy(panel_ref, own, isem.at[0])
    load_contrib = pltpu.make_async_copy(contribution_ref, contrib, isem.at[1])
    barrier = pltpu.get_barrier_semaphore()
    for device in (to_x, to_core, to_row):
        pl.semaphore_signal(barrier, inc=1, device_id=device, device_id_type=MESH)
    pl.semaphore_wait(barrier, 3)

    def spot(rr, cc):
        return a_ref.at[pl.ds(pl.multiple_of((rr * 4 + cc) * ndiag, ndiag), ndiag)]

    def diag_copy(k, src, rr, cc, device):
        return remote(src, spot(rr, cc), dsend.at[k], drecv.at[k], device)

    def across(i):
        part = pl.ds(pl.multiple_of(i * rows, rows), rows)
        return remote(panel_ref.at[part], g1.at[part], xsend.at[i], xrecv.at[i], to_x)

    def onward(i):
        part = pl.ds(pl.multiple_of(i * rows, rows), rows)
        return remote(g1.at[part], g2.at[part], fsend.at[i], frecv.at[i], to_core)

    own_piece = remote(panel_ref, g0, psend, precv, to_core)
    mask_x = remote(mask_ref, masks.at[2], msend.at[0], mrecv.at[0], to_x)
    mask_core = remote(mask_ref, masks.at[1], msend.at[1], mrecv.at[1], to_core)
    mask_on = remote(masks.at[2], masks.at[3], msend.at[2], mrecv.at[2], to_core)

    first = diag_copy(0, diag_ref, r, c, to_x)
    first.start()
    mask_x.start()
    for i in range(chunks):
        across(i).start()
    second = [diag_copy(1, diag_ref, r, c, to_row)]
    second[0].start()
    mask_core.start()
    load_own.start()
    load_contrib.start()
    a_ref[pl.ds(pl.multiple_of((r * 4 + c) * ndiag, ndiag), ndiag), :] = diag_ref[...]
    masks[0] = mask_ref[...]
    first.wait_recv()
    second.append(diag_copy(2, spot(r, c2), r, c2, to_row))
    second[1].start()
    third = [
        diag_copy(3, diag_ref, r, c, to_core),
        diag_copy(4, spot(r, c2), r, c2, to_core),
    ]
    for copy in third:
        copy.start()
    mask_x.wait_recv()
    mask_on.start()
    for copy in second:
        copy.wait_recv()
    third.append(diag_copy(5, spot(y, c), y, c, to_core))
    third.append(diag_copy(6, spot(y, c2), y, c2, to_core))
    for copy in third[2:]:
        copy.start()
    for copy in third:
        copy.wait_recv()
    for copy in [first] + second + third:
        copy.wait_send()
    own_piece.start()

    ahead = chunks // 2

    def between(p):
        for i in range(p * ahead // 4, (p + 1) * ahead // 4):
            across(i).wait_recv()
            onward(i).start()

    cholesky_inverse(a_ref, inv_ref, s_ref, x_ref, between)
    l_ref[...] = a_ref[pl.ds(pl.multiple_of((r * 4 + c) * ndiag, ndiag), ndiag), :]

    load_own.wait()
    load_contrib.wait()
    own_piece.wait_recv()
    mask_core.wait_recv()
    mask_on.wait_recv()
    early = max(1, 4 * BS // rows)
    for i in range(early):
        onward(i).wait_recv()
    head = remote(h_ref, h_ref, hsend.at[0], hrecv.at[0], to_row)
    head_mask = remote(masks, head_masks, hsend.at[1], hrecv.at[1], to_row)
    window = pl.ds(pl.multiple_of(c * BS, BS), BS)

    @pl.when(r == 0)
    def _():
        loads = [
            pltpu.make_async_copy(piece.at[window], h_ref.at[j], lsem.at[j])
            for j, piece in enumerate(pieces)
        ]
        for copy in loads:
            copy.start()
        for copy in loads:
            copy.wait()
        head.start()
        head_mask.start()
        for j, k in enumerate(order):
            hc_ref[:, pl.ds(pl.multiple_of(k * BS, BS), BS)] = h_ref[j] * masks[j, pl.ds(c, 1), :]
        head.wait_send()
        head_mask.wait_send()

    @pl.when(r == 1)
    def _():
        head.wait_recv()
        head_mask.wait_recv()
        for j, k in enumerate(order):
            hc_ref[:, pl.ds(pl.multiple_of(k * BS, BS), BS)] = h_ref[j] * head_masks[j, pl.ds(c, 1), :]

    factor_head = lax.dot_general(hc_ref[...], inv_ref[...], NT, precision=HIGHEST)
    w_ref[pl.ds(BS, BS), :] = jnp.dot(factor_head, inv_ref[...], precision=HIGHEST)
    w_ref[pl.ds(0, BS), :] = inv_ref[pl.ds(pl.multiple_of(c * BS, BS), BS), :]
    for j, k in enumerate(order):
        high, low = split(jnp.transpose(w_ref[:, pl.ds(pl.multiple_of(k * BS, BS), BS)]))
        vh_ref[j * BS:(j + 1) * BS, :] = high
        vl_ref[j * BS:(j + 1) * BS, :] = low

    def stores(i, buf):
        part = pl.ds(pl.multiple_of(i * rows, rows), rows)
        return (
            pltpu.make_async_copy(fs.at[buf], f_ref.at[part], osem.at[0, buf]),
            pltpu.make_async_copy(us.at[buf], u_ref.at[part], osem.at[1, buf]),
        )

    def compute(i):
        buf = i % 2

        @pl.when(i >= 2)
        def _():
            for copy in stores(i - 2, buf):
                copy.wait()

        start = pl.multiple_of(i * rows, rows)
        blocks = []
        for b in range(rows // BS):
            part = pl.ds(pl.multiple_of(start + b * BS, BS), BS)
            at = i * (rows // BS) + b
            blocks.append(jnp.concatenate(
                [piece[part, :] * masks[j, pl.ds(at, 1), :] for j, piece in enumerate(pieces)], axis=1))
        high, low = split(jnp.concatenate(blocks, axis=0))
        dot = functools.partial(jnp.dot, preferred_element_type=jnp.float32)
        out = dot(high, vh_ref[...]) + (dot(high, vl_ref[...]) + dot(low, vh_ref[...]))
        fs[buf] = out[:, :BS]
        us[buf] = contrib[pl.ds(start, rows), :] - out[:, BS:]
        for copy in stores(i, buf):
            copy.start()

    def step(i, carry):
        @pl.when((i >= ahead) & (i < chunks))
        def _():
            across(i).wait_recv()
            onward(i).start()

        @pl.when(i > early)
        def _():
            onward(i - 1).wait_recv()

        @pl.when(i > 0)
        def _():
            compute(i - 1)
        return carry

    lax.fori_loop(0, chunks + 1, step, 0)
    for i in (chunks - 2, chunks - 1):
        for copy in stores(i, i % 2):
            copy.wait()
    for i in range(chunks):
        across(i).wait_send()
        onward(i).wait_send()
    own_piece.wait_send()
    for copy in (mask_x, mask_core, mask_on):
        copy.wait_send()


def gather_and_factor(diag, mask, panel, contribution):
    chunks = 16
    rows, share = panel.shape
    tile = rows // chunks
    ndiag, width = diag.shape
    piece = jax.ShapeDtypeStruct((rows, share), jnp.float32)
    whole = pltpu.VMEM((rows, share), jnp.float32)
    square = pltpu.VMEM((width, width), jnp.float32)
    block = pltpu.VMEM((BS, BS), jnp.float32)
    sems = pltpu.SemaphoreType.DMA
    return pl.pallas_call(
        functools.partial(gather_kernel, chunks),
        out_shape=(piece, piece, jax.ShapeDtypeStruct((ndiag, width), jnp.float32)),
        in_specs=[VMEM, VMEM, ANY, ANY],
        out_specs=(ANY, ANY, VMEM),
        scratch_shapes=[
            whole, whole, whole, whole, whole,
            square, square, block, block,
            pltpu.VMEM((4, BS, BS), jnp.float32),
            pltpu.VMEM((BS, width), jnp.float32),
            pltpu.VMEM((2 * BS, width), jnp.float32),
            pltpu.VMEM((width, 2 * BS), jnp.bfloat16),
            pltpu.VMEM((width, 2 * BS), jnp.bfloat16),
            pltpu.VMEM((4,) + mask.shape, jnp.float32),
            pltpu.VMEM((4,) + mask.shape, jnp.float32),
            pltpu.VMEM((2, tile, share), jnp.float32),
            pltpu.VMEM((2, tile, share), jnp.float32),
            sems((7,)), sems((7,)),
            sems((chunks,)), sems((chunks,)), sems((chunks,)), sems((chunks,)),
            sems, sems, sems((2,)), sems((2,)), sems((3,)), sems((3,)),
            sems((4,)), sems((2,)), sems((2, 2)),
        ],
        compiler_params=pltpu.CompilerParams(
            collective_id=0, has_side_effects=True, vmem_limit_bytes=48 * 2**20),
        name="gather_factor",
    )(diag, mask, panel, contribution)


def split(value):
    high = value.astype(jnp.bfloat16)
    return high, (value - high.astype(jnp.float32)).astype(jnp.bfloat16)


def pack_kernel(tile, pblk, route_ref, slot_ref, f_in, u_ref, f_ref, t_ref):
    step = pl.program_id(0)

    @pl.when(step == 0)
    def _():
        t_ref[...] = jnp.zeros_like(t_ref)

    f_ref[...] = f_in[...]
    for b in range(tile // BS):
        at = step * (tile // BS) + b
        goal = route_ref[at] * pblk + slot_ref[at]
        t_ref[goal] = t_ref[goal] + u_ref[b * BS:(b + 1) * BS, :]


def pack_blocks(route, slot, factor, update, slots, pblk):
    tile = 1024
    rows, share = factor.shape
    block = pl.BlockSpec((tile, share), lambda i, g, s: (i, 0))
    return pl.pallas_call(
        functools.partial(pack_kernel, tile, pblk),
        out_shape=(
            jax.ShapeDtypeStruct((rows, share), jnp.float32),
            jax.ShapeDtypeStruct((slots, BS, share), jnp.float32),
        ),
        grid_spec=pltpu.PrefetchScalarGridSpec(
            num_scalar_prefetch=2,
            grid=(rows // tile,),
            in_specs=[block] * 2,
            out_specs=(block, pl.BlockSpec((slots, BS, share), lambda i, g, s: (0, 0, 0))),
        ),
        compiler_params=pltpu.CompilerParams(dimension_semantics=("arbitrary",)),
        name="pack_blocks",
    )(route, slot, factor, update)


def route_kernel(t_ref, out_ref, ra, rb, ra2, rb2, asend, arecv, bsend, brecv,
                 a2send, a2recv, b2send, b2recv):
    z, r = lax.axis_index("cube"), lax.axis_index("row")
    m, y = z % 2, 1 - r
    dev_y = {"row": y}
    dev_z = {"cube": z + 1 - 2 * m}
    barrier = pltpu.get_barrier_semaphore()
    for device in (dev_y, dev_z):
        pl.semaphore_signal(barrier, inc=1, device_id=device, device_id_type=MESH)
    pl.semaphore_wait(barrier, 2)
    half = t_ref.shape[1] // 2
    n = 8
    parts = half // n
    over_a, over_b = {}, {}
    for rel in range(2):
        for k in range(parts):
            h = (1 - m) if rel == 0 else m
            over_a[rel, k] = remote(
                t_ref.at[h * 2 + y, pl.ds(k * n, n)], ra.at[rel, pl.ds(k * n, n)],
                asend.at[rel, k], arecv.at[rel, k], dev_y)
            rr = y if rel == 0 else r
            over_b[rel, k] = remote(
                t_ref.at[(1 - m) * 2 + rr, pl.ds(half + k * n, n)], rb.at[rel, pl.ds(k * n, n)],
                bsend.at[rel, k], brecv.at[rel, k], dev_z)
            over_a[rel, k].start()
            over_b[rel, k].start()
    last = {}
    for k in range(parts):
        part = pl.ds(k * n, n)
        other = pl.ds(half + k * n, n)
        over_a[0, k].wait_recv()
        ra[0, part] = ra[0, part] + t_ref[(1 - m) * 2 + r, part]
        over_b[0, k].wait_recv()
        rb[0, part] = rb[0, part] + t_ref[m * 2 + y, other]
        last[0, k] = remote(ra.at[0, part], ra2.at[part], a2send.at[k], a2recv.at[k], dev_z)
        last[1, k] = remote(rb.at[0, part], rb2.at[part], b2send.at[k], b2recv.at[k], dev_y)
        last[0, k].start()
        last[1, k].start()
    for k in range(parts):
        part = pl.ds(k * n, n)
        other = pl.ds(half + k * n, n)
        over_a[1, k].wait_recv()
        out_ref[part] = t_ref[m * 2 + r, part] + ra[1, part]
        over_b[1, k].wait_recv()
        out_ref[other] = t_ref[m * 2 + r, other] + rb[1, part]
    for k in range(parts):
        part = pl.ds(k * n, n)
        other = pl.ds(half + k * n, n)
        last[0, k].wait_recv()
        out_ref[part] = out_ref[part] + ra2[part]
        last[1, k].wait_recv()
        out_ref[other] = out_ref[other] + rb2[part]
    for copy in list(over_a.values()) + list(over_b.values()) + list(last.values()):
        copy.wait_send()


def route_blocks(packed):
    _, slots, rows, share = packed.shape
    half = slots // 2
    parts = half // 8
    return pl.pallas_call(
        route_kernel,
        out_shape=jax.ShapeDtypeStruct((slots, rows, share), jnp.float32),
        in_specs=[VMEM],
        out_specs=VMEM,
        scratch_shapes=[
            pltpu.VMEM((2, half, rows, share), jnp.float32),
            pltpu.VMEM((2, half, rows, share), jnp.float32),
            pltpu.VMEM((half, rows, share), jnp.float32),
            pltpu.VMEM((half, rows, share), jnp.float32),
            pltpu.SemaphoreType.DMA((2, parts)),
            pltpu.SemaphoreType.DMA((2, parts)),
            pltpu.SemaphoreType.DMA((2, parts)),
            pltpu.SemaphoreType.DMA((2, parts)),
            pltpu.SemaphoreType.DMA((parts,)),
            pltpu.SemaphoreType.DMA((parts,)),
            pltpu.SemaphoreType.DMA((parts,)),
            pltpu.SemaphoreType.DMA((parts,)),
        ],
        compiler_params=pltpu.CompilerParams(collective_id=1, has_side_effects=True),
        name="route_blocks",
    )(packed)


def on_small(diag_block, panel, pattern, contribution, route, slot):
    rows, share = panel.shape[1:]
    blk = rows // BS
    pblk = blk // 2
    nrow = lax.axis_size("row")
    mask = jnp.broadcast_to(pattern[0].astype(jnp.float32), (blk, share))
    factor, update, lower = gather_and_factor(diag_block[0], mask, panel[0], contribution[0])
    factor, packed = pack_blocks(route[0, :, 0], slot[0], factor, update, 2 * nrow * pblk, pblk)
    assembled = route_blocks(packed.reshape(2 * nrow, pblk, BS, share))
    return (lower[None], factor[None], assembled.reshape(1, pblk * BS, share))


def from_root(value, axis, root):
    mine = lax.axis_index(axis) == root
    return lax.psum(jnp.where(mine, value, jnp.zeros_like(value)), axis)


def partner(value, axis, apart):
    mask = 2**apart
    pairs = [(source, source ^ mask) for source in range(lax.axis_size(axis))]
    return lax.ppermute(value, axis, pairs)


def on_large(diag_block, panel, pattern, contribution, route, slot):
    highest = lax.Precision.HIGHEST
    contract = (((1,), (1,)), ((), ()))
    whole = lax.all_gather(diag_block, ("row", "col"), axis=1, tiled=True)[0]
    width = whole.shape[0]
    lower = jnp.linalg.cholesky(whole)
    inverse = jax.scipy.linalg.solve_triangular(
        lower, jnp.eye(width, dtype=jnp.float32), lower=True
    )
    ncol = lax.axis_size("col")
    nrow = lax.axis_size("row")
    col_index = lax.axis_index("col")
    tile_mask = jnp.repeat(jnp.repeat(pattern[0], BS, axis=0), BS, axis=1).astype(jnp.float32)
    masked = panel[0] * tile_mask
    rows_dev = masked.shape[0]
    full_rows = lax.all_gather(masked, "col", axis=1, tiled=True)
    factor_rows = lax.dot_general(full_rows, inverse, contract, precision=highest)
    share = width // ncol
    own_cols = lax.dynamic_slice_in_dim(factor_rows, col_index * share, share, 1)
    cw_dev = contribution.shape[2]
    head_piece = lax.dynamic_slice_in_dim(factor_rows, col_index * cw_dev, cw_dev, 0)
    head_rows = from_root(head_piece, "row", 0)
    update = contribution[0] - lax.dot_general(factor_rows, head_rows, contract, precision=highest)
    blk = rows_dev // BS
    cap = max(2, blk // nrow)
    pblk = blk // 2
    blocks = update.reshape(blk, BS * cw_dev)
    target = route[0, :, 0]
    place = slot[0]
    order_ids = jnp.arange(blk, dtype=jnp.int32)
    earlier = (target[None, :] == target[:, None]) & (order_ids[None, :] < order_ids[:, None])
    rank = jnp.sum(earlier.astype(jnp.int32), axis=1)
    half = target // nrow
    target_row = target % nrow
    position = target_row * (2 * cap) + half * cap + rank
    slots_all = jnp.arange(nrow * 2 * cap, dtype=jnp.int32)
    onehot = (position[None, :] == slots_all[:, None]).astype(jnp.float32)
    packed = jnp.dot(onehot, blocks, precision=highest).reshape(nrow, 2, cap, BS * cw_dev)
    labels = jnp.dot(onehot, (place + 1).astype(jnp.float32), precision=highest).reshape(
        nrow, 2, cap
    )
    mine = lax.axis_index("cube") % 2
    got, got_labels = (
        lax.all_to_all(packed, "row", split_axis=0, concat_axis=0, tiled=True),
        lax.all_to_all(labels, "row", split_axis=0, concat_axis=0, tiled=True),
    )
    keep = lax.dynamic_index_in_dim(got, mine, 1, keepdims=False)
    keep_labels = lax.dynamic_index_in_dim(got_labels, mine, 1, keepdims=False)
    other = lax.dynamic_index_in_dim(got, 1 - mine, 1, keepdims=False)
    other_labels = lax.dynamic_index_in_dim(got_labels, 1 - mine, 1, keepdims=False)
    back, back_labels = partner((other, other_labels), "cube", 0)
    incoming = jnp.concatenate([keep, back], axis=0).reshape(-1, BS * cw_dev)
    tags = jnp.concatenate([keep_labels, back_labels], axis=0).reshape(-1)
    wanted = jnp.arange(1, pblk + 1, dtype=jnp.float32)
    select = (tags[None, :] == wanted[:, None]).astype(jnp.float32)
    assembled = jnp.dot(select, incoming, precision=highest).reshape(pblk * BS, cw_dev)
    rows_here = diag_block.shape[1]
    diag_rows = lax.dynamic_slice_in_dim(
        lower, lax.axis_index(("row", "col")) * rows_here, rows_here, 0
    )
    return (diag_rows[None], own_cols[None], assembled[None])


def solution(mesh):
    small = mesh.shape["row"] == 2 and mesh.shape["col"] == 4
    return jax.shard_map(
        on_small if small else on_large,
        mesh=mesh,
        in_specs=(
            P("cube", ("row", "col"), None),
            P("cube", "row", "col"),
            P("cube", "row", "col"),
            P("cube", "row", "col"),
            P("cube", "row", None),
            P("cube", "row"),
        ),
        out_specs=(
            P("cube", ("row", "col"), None),
            P("cube", "row", "col"),
            P("cube", "row", "col"),
        ),
        check_vma=False,
    )
```

```python
import functools

import jax
import jax.numpy as jnp
from jax import lax
from jax.experimental import pallas as pl
from jax.experimental.pallas import tpu as pltpu
from jax.sharding import PartitionSpec as P

BS = 128
HIGHEST = lax.Precision.HIGHEST
NT = (((1,), (1,)), ((), ()))
ANY = pl.BlockSpec(memory_space=pl.ANY)
VMEM = pl.BlockSpec(memory_space=pltpu.VMEM)
SMEM = pl.BlockSpec(memory_space=pltpu.SMEM)
MESH = pl.DeviceIdType.MESH


def remote(src, dst, send, recv, device):
    return pltpu.make_async_remote_copy(
        src_ref=src, dst_ref=dst, send_sem=send, recv_sem=recv,
        device_id=device, device_id_type=MESH,
    )


def factor_block(s_ref, x_ref):
    n = BS
    sub = lax.broadcasted_iota(jnp.int32, (n, n), 0)
    lane = lax.broadcasted_iota(jnp.int32, (n, n), 1)
    x_ref[...] = (sub == lane).astype(jnp.float32)
    step = 32
    for lo in range(0, n, step):
        rows = n - lo
        lane_r = lax.broadcasted_iota(jnp.int32, (rows, n), 1)
        sub_c = lax.broadcasted_iota(jnp.int32, (rows, 1), 0) + lo
        lane_1 = lax.broadcasted_iota(jnp.int32, (1, n), 1)

        def body(j, carry):
            s = s_ref[pl.ds(lo, rows), :]
            x = x_ref[pl.ds(lo, rows), :]
            row_s = s_ref[pl.ds(j, 1), :]
            row_x = x_ref[pl.ds(j, 1), :]
            col = jnp.sum(jnp.where(lane_r == j, s, 0.0), axis=1, keepdims=True)
            pivot = jnp.sum(jnp.where(lane_1 == j, row_s, 0.0), axis=1, keepdims=True)
            scale = 1.0 / pivot
            col = jnp.where(sub_c > j, col, 0.0)
            s_ref[pl.ds(lo, rows), :] = s - col * (row_s * scale)
            x_ref[pl.ds(lo, rows), :] = x - col * (row_x * scale)
            return carry

        lax.fori_loop(lo, lo + step, body, 0)


def cholesky_inverse(a_ref, inv_ref, s_ref, x_ref, between):
    width = a_ref.shape[0]
    sub = lax.broadcasted_iota(jnp.int32, (BS, BS), 0)
    lane = lax.broadcasted_iota(jnp.int32, (BS, BS), 1)
    inv_ref[...] = jnp.zeros_like(inv_ref)
    for p in range(width // BS):
        o, e = p * BS, (p + 1) * BS
        s_ref[...] = a_ref[o:e, o:e]
        factor_block(s_ref, x_ref)
        s = s_ref[...]
        d = jnp.sum(jnp.where(lane == sub, s, 0.0), axis=1, keepdims=True)
        rs = 1.0 / jnp.sqrt(d)
        low = jnp.transpose(jnp.where(lane >= sub, s, 0.0) * rs)
        x = x_ref[...] * rs
        a_ref[o:e, o:e] = low
        inv_ref[o:e, o:e] = x
        if e < width:
            below = lax.dot_general(a_ref[e:, o:e], x, NT, precision=HIGHEST)
            a_ref[e:, o:e] = below
            a_ref[e:, e:] = a_ref[e:, e:] - lax.dot_general(below, below, NT, precision=HIGHEST)
            a_ref[o:e, e:] = jnp.zeros((BS, width - e), jnp.float32)
        if p > 0:
            part = jnp.dot(a_ref[o:e, :o], inv_ref[:o, :o], precision=HIGHEST)
            inv_ref[o:e, :o] = -jnp.dot(x, part, precision=HIGHEST)
        between(p)


def gather_kernel(chunks, prev_ref, prev_on, last_ref, last_on, diag_ref, mask_ref, panel_ref, contribution_ref, f_ref, out_ref, l_ref,
                  own, g0, g1, g2, contrib, a_ref, inv_ref, s_ref, x_ref, h_ref, hc_ref, w_ref,
                  vh_ref, vl_ref, masks, head_masks, fs, t_ref, ra, rb, ra2, rb2,
                  dsend, drecv, xsend, xrecv, fsend, frecv, psend, precv, hsend, hrecv,
                  msend, mrecv, lsem, isem, osem,
                  asend, arecv, bsend, brecv, a2send, a2recv, b2send, b2recv):
    z = lax.axis_index("cube")
    m = z % 2
    r, c = lax.axis_index("row"), lax.axis_index("col")
    y = 1 - r
    c1 = c + 1 - 2 * (c % 2)
    c2 = (c + 2) % 4
    c3 = (c1 + 2) % 4
    order = (c, c1, c2, c3)
    pieces = (own, g0, g1, g2)
    ndiag = diag_ref.shape[0]
    rows = panel_ref.shape[0] // chunks
    to_x, to_core, to_row = {"col": c2}, {"col": c1}, {"row": y}

    load_own = pltpu.make_async_copy(panel_ref, own, isem.at[0])
    load_contrib = pltpu.make_async_copy(contribution_ref, contrib, isem.at[1])
    barrier = pltpu.get_barrier_semaphore()
    to_cube = {"cube": z + 1 - 2 * m}
    for device in (to_x, to_core, to_row, to_cube):
        pl.semaphore_signal(barrier, inc=1, device_id=device, device_id_type=MESH)
    pl.semaphore_wait(barrier, 4)

    def spot(rr, cc):
        return a_ref.at[pl.ds(pl.multiple_of((rr * 4 + cc) * ndiag, ndiag), ndiag)]

    def diag_copy(k, src, rr, cc, device):
        return remote(src, spot(rr, cc), dsend.at[k], drecv.at[k], device)

    def across(i):
        part = pl.ds(pl.multiple_of(i * rows, rows), rows)
        return remote(panel_ref.at[part], g1.at[part], xsend.at[i], xrecv.at[i], to_x)

    def onward(i):
        part = pl.ds(pl.multiple_of(i * rows, rows), rows)
        return remote(g1.at[part], g2.at[part], fsend.at[i], frecv.at[i], to_core)

    own_piece = remote(panel_ref, g0, psend, precv, to_core)
    mask_x = remote(mask_ref, masks.at[2], msend.at[0], mrecv.at[0], to_x)
    mask_core = remote(mask_ref, masks.at[1], msend.at[1], mrecv.at[1], to_core)
    mask_on = remote(masks.at[2], masks.at[3], msend.at[2], mrecv.at[2], to_core)

    first = diag_copy(0, diag_ref, r, c, to_x)
    first.start()
    mask_x.start()
    for i in range(chunks):
        across(i).start()
    second = [diag_copy(1, diag_ref, r, c, to_row)]
    second[0].start()
    mask_core.start()
    load_own.start()
    load_contrib.start()
    a_ref[pl.ds(pl.multiple_of((r * 4 + c) * ndiag, ndiag), ndiag), :] = diag_ref[...]
    masks[0] = mask_ref[...]
    first.wait_recv()
    second.append(diag_copy(2, spot(r, c2), r, c2, to_row))
    second[1].start()
    third = [
        diag_copy(3, diag_ref, r, c, to_core),
        diag_copy(4, spot(r, c2), r, c2, to_core),
    ]
    for copy in third:
        copy.start()
    mask_x.wait_recv()
    mask_on.start()
    for copy in second:
        copy.wait_recv()
    third.append(diag_copy(5, spot(y, c), y, c, to_core))
    third.append(diag_copy(6, spot(y, c2), y, c2, to_core))
    for copy in third[2:]:
        copy.start()
    for copy in third:
        copy.wait_recv()
    for copy in [first] + second + third:
        copy.wait_send()
    own_piece.start()

    ahead = chunks // 2

    def between(p):
        for i in range(p * ahead // 4, (p + 1) * ahead // 4):
            across(i).wait_recv()
            onward(i).start()

    cholesky_inverse(a_ref, inv_ref, s_ref, x_ref, between)
    l_ref[...] = a_ref[pl.ds(pl.multiple_of((r * 4 + c) * ndiag, ndiag), ndiag), :]

    load_own.wait()
    load_contrib.wait()
    own_piece.wait_recv()
    mask_core.wait_recv()
    mask_on.wait_recv()
    early = max(1, 4 * BS // rows)
    for i in range(early):
        onward(i).wait_recv()
    head = remote(h_ref, h_ref, hsend.at[0], hrecv.at[0], to_row)
    head_mask = remote(masks, head_masks, hsend.at[1], hrecv.at[1], to_row)
    window = pl.ds(pl.multiple_of(c * BS, BS), BS)

    @pl.when(r == 0)
    def _():
        loads = [
            pltpu.make_async_copy(piece.at[window], h_ref.at[j], lsem.at[j])
            for j, piece in enumerate(pieces)
        ]
        for copy in loads:
            copy.start()
        for copy in loads:
            copy.wait()
        head.start()
        head_mask.start()
        for j, k in enumerate(order):
            hc_ref[:, pl.ds(pl.multiple_of(k * BS, BS), BS)] = h_ref[j] * masks[j, pl.ds(c, 1), :]
        head.wait_send()
        head_mask.wait_send()

    @pl.when(r == 1)
    def _():
        head.wait_recv()
        head_mask.wait_recv()
        for j, k in enumerate(order):
            hc_ref[:, pl.ds(pl.multiple_of(k * BS, BS), BS)] = h_ref[j] * head_masks[j, pl.ds(c, 1), :]

    factor_head = lax.dot_general(hc_ref[...], inv_ref[...], NT, precision=HIGHEST)
    w_ref[pl.ds(BS, BS), :] = jnp.dot(factor_head, inv_ref[...], precision=HIGHEST)
    w_ref[pl.ds(0, BS), :] = inv_ref[pl.ds(pl.multiple_of(c * BS, BS), BS), :]
    for j, k in enumerate(order):
        high, low = split(jnp.transpose(w_ref[:, pl.ds(pl.multiple_of(k * BS, BS), BS)]))
        vh_ref[j * BS:(j + 1) * BS, :] = high
        vl_ref[j * BS:(j + 1) * BS, :] = low

    def stores(i, buf):
        part = pl.ds(pl.multiple_of(i * rows, rows), rows)
        return (pltpu.make_async_copy(fs.at[buf], f_ref.at[part], osem.at[buf]),)

    def compute(i):
        buf = i % 2

        @pl.when(i >= 2)
        def _():
            for copy in stores(i - 2, buf):
                copy.wait()

        start = pl.multiple_of(i * rows, rows)
        blocks = []
        for b in range(rows // BS):
            part = pl.ds(pl.multiple_of(start + b * BS, BS), BS)
            at = i * (rows // BS) + b
            blocks.append(jnp.concatenate(
                [piece[part, :] * masks[j, pl.ds(at, 1), :] for j, piece in enumerate(pieces)], axis=1))
        high, low = split(jnp.concatenate(blocks, axis=0))
        dot = functools.partial(jnp.dot, preferred_element_type=jnp.float32)
        out = dot(high, vh_ref[...]) + (dot(high, vl_ref[...]) + dot(low, vh_ref[...]))
        fs[buf] = out[:, :BS]
        for copy in stores(i, buf):
            copy.start()
        for b in range(rows // BS):
            at = i * (rows // BS) + b
            update = contrib[at] - out[b * BS:(b + 1) * BS, BS:]
            contrib[at] = update + prev_on[at] * contrib[prev_ref[at]]

    def step(i, carry):
        @pl.when((i >= ahead) & (i < chunks))
        def _():
            across(i).wait_recv()
            onward(i).start()

        @pl.when(i > early)
        def _():
            onward(i - 1).wait_recv()

        @pl.when(i > 0)
        def _():
            compute(i - 1)
        return carry

    lax.fori_loop(0, chunks + 1, step, 0)
    slots = out_ref.shape[0]

    def fill(h, rr, begin, end):
        def body(k, carry):
            name = (h * 2 + rr) * slots + k
            t_ref[h * 2 + rr, k] = contrib[last_ref[name]] * last_on[name]
            return carry

        lax.fori_loop(begin, end, body, 0)

    route_slots(m, r, y, to_row, to_cube, fill, t_ref, out_ref, ra, rb, ra2, rb2,
                asend, arecv, bsend, brecv, a2send, a2recv, b2send, b2recv)
    for i in (chunks - 2, chunks - 1):
        for copy in stores(i, i % 2):
            copy.wait()
    for i in range(chunks):
        across(i).wait_send()
        onward(i).wait_send()
    own_piece.wait_send()
    for copy in (mask_x, mask_core, mask_on):
        copy.wait_send()


def factor_and_route(chains, diag, mask, panel, contribution, pblk):
    chunks = 16
    rows, share = panel.shape
    tile = rows // chunks
    half = pblk // 2
    parts = half // 4
    ndiag, width = diag.shape
    piece = jax.ShapeDtypeStruct((rows, share), jnp.float32)
    whole = pltpu.VMEM((rows, share), jnp.float32)
    square = pltpu.VMEM((width, width), jnp.float32)
    block = pltpu.VMEM((BS, BS), jnp.float32)
    sems = pltpu.SemaphoreType.DMA
    return pl.pallas_call(
        functools.partial(gather_kernel, chunks),
        out_shape=(
            piece,
            jax.ShapeDtypeStruct((pblk, BS, share), jnp.float32),
            jax.ShapeDtypeStruct((ndiag, width), jnp.float32),
        ),
        in_specs=[SMEM, SMEM, SMEM, SMEM, VMEM, VMEM, ANY, ANY],
        out_specs=(ANY, VMEM, VMEM),
        scratch_shapes=[
            whole, whole, whole, whole, pltpu.VMEM((rows // BS, BS, share), jnp.float32),
            square, square, block, block,
            pltpu.VMEM((4, BS, BS), jnp.float32),
            pltpu.VMEM((BS, width), jnp.float32),
            pltpu.VMEM((2 * BS, width), jnp.float32),
            pltpu.VMEM((width, 2 * BS), jnp.bfloat16),
            pltpu.VMEM((width, 2 * BS), jnp.bfloat16),
            pltpu.VMEM((4,) + mask.shape, jnp.float32),
            pltpu.VMEM((4,) + mask.shape, jnp.float32),
            pltpu.VMEM((2, tile, share), jnp.float32),
            pltpu.VMEM((4, pblk, BS, share), jnp.float32),
            pltpu.VMEM((2, half, BS, share), jnp.float32),
            pltpu.VMEM((2, half, BS, share), jnp.float32),
            pltpu.VMEM((half, BS, share), jnp.float32),
            pltpu.VMEM((half, BS, share), jnp.float32),
            sems((7,)), sems((7,)),
            sems((chunks,)), sems((chunks,)), sems((chunks,)), sems((chunks,)),
            sems, sems, sems((2,)), sems((2,)), sems((3,)), sems((3,)),
            sems((4,)), sems((2,)), sems((2,)),
            sems((2, parts)), sems((2, parts)), sems((2, parts)), sems((2, parts)),
            sems((parts,)), sems((parts,)), sems((parts,)), sems((parts,)),
        ],
        compiler_params=pltpu.CompilerParams(
            collective_id=0, has_side_effects=True, vmem_limit_bytes=58 * 2**20),
        name="gather_factor",
    )(*chains, diag, mask, panel, contribution.reshape(rows // BS, BS, share))


def split(value):
    high = value.astype(jnp.bfloat16)
    return high, (value - high.astype(jnp.float32)).astype(jnp.bfloat16)


def route_slots(m, r, y, dev_y, dev_z, fill, t_ref, out_ref, ra, rb, ra2, rb2,
                asend, arecv, bsend, brecv, a2send, a2recv, b2send, b2recv):
    slots = t_ref.shape[1]
    half = slots // 2
    n = 4
    parts = half // n
    over_a, over_b, last = {}, {}, {}
    for rel in range(2):
        for k in range(parts):
            h = (1 - m) if rel == 0 else m
            over_a[rel, k] = remote(
                t_ref.at[h * 2 + y, pl.ds(k * n, n)], ra.at[rel, pl.ds(k * n, n)],
                asend.at[rel, k], arecv.at[rel, k], dev_y)
            rr = y if rel == 0 else r
            over_b[rel, k] = remote(
                t_ref.at[(1 - m) * 2 + rr, pl.ds(half + k * n, n)], rb.at[rel, pl.ds(k * n, n)],
                bsend.at[rel, k], brecv.at[rel, k], dev_z)
    fill(1 - m, y, 0, slots)
    for k in range(parts):
        over_a[0, k].start()
        over_b[0, k].start()
    fill(m, y, 0, slots)
    fill(1 - m, r, 0, slots)
    for k in range(parts):
        over_a[1, k].start()
        over_b[1, k].start()
    fill(m, r, 0, slots)
    for k in range(parts):
        part = pl.ds(k * n, n)
        other = pl.ds(half + k * n, n)
        over_a[0, k].wait_recv()
        ra[0, part] = ra[0, part] + t_ref[(1 - m) * 2 + r, part]
        over_b[0, k].wait_recv()
        rb[0, part] = rb[0, part] + t_ref[m * 2 + y, other]
        last[0, k] = remote(ra.at[0, part], ra2.at[part], a2send.at[k], a2recv.at[k], dev_z)
        last[1, k] = remote(rb.at[0, part], rb2.at[part], b2send.at[k], b2recv.at[k], dev_y)
        last[0, k].start()
        last[1, k].start()
    for k in range(parts):
        part = pl.ds(k * n, n)
        other = pl.ds(half + k * n, n)
        over_a[1, k].wait_recv()
        out_ref[part] = t_ref[m * 2 + r, part] + ra[1, part]
        over_b[1, k].wait_recv()
        out_ref[other] = t_ref[m * 2 + r, other] + rb[1, part]
    for k in range(parts):
        part = pl.ds(k * n, n)
        other = pl.ds(half + k * n, n)
        last[0, k].wait_recv()
        out_ref[part] = out_ref[part] + ra2[part]
        last[1, k].wait_recv()
        out_ref[other] = out_ref[other] + rb2[part]
    for copy in list(over_a.values()) + list(over_b.values()) + list(last.values()):
        copy.wait_send()


def on_small(diag_block, panel, pattern, contribution, route, slot):
    rows, share = panel.shape[1:]
    blk = rows // BS
    pblk = blk // 2
    nrow = lax.axis_size("row")
    mask = jnp.broadcast_to(pattern[0].astype(jnp.float32), (blk, share))
    goal = (route[0, :, 0] * pblk + slot[0]).astype(jnp.int32)
    ids = jnp.arange(blk, dtype=jnp.int32)
    earlier = (goal[None, :] == goal[:, None]) & (ids[None, :] < ids[:, None])
    prev = jnp.max(jnp.where(earlier, ids[None, :] + 1, 0), axis=1)
    names = jnp.arange(2 * nrow * pblk, dtype=jnp.int32)
    last = jnp.max(jnp.where(goal[None, :] == names[:, None], ids[None, :] + 1, 0), axis=1)
    chains = (
        jnp.maximum(prev - 1, 0), jnp.minimum(prev, 1).astype(jnp.float32),
        jnp.maximum(last - 1, 0), jnp.minimum(last, 1).astype(jnp.float32),
    )
    factor, assembled, lower = factor_and_route(
        chains, diag_block[0], mask, panel[0], contribution[0], pblk)
    return (lower[None], factor[None], assembled.reshape(1, pblk * BS, share))


def from_root(value, axis, root):
    mine = lax.axis_index(axis) == root
    return lax.psum(jnp.where(mine, value, jnp.zeros_like(value)), axis)


def partner(value, axis, apart):
    mask = 2**apart
    pairs = [(source, source ^ mask) for source in range(lax.axis_size(axis))]
    return lax.ppermute(value, axis, pairs)


def on_large(diag_block, panel, pattern, contribution, route, slot):
    highest = lax.Precision.HIGHEST
    contract = (((1,), (1,)), ((), ()))
    whole = lax.all_gather(diag_block, ("row", "col"), axis=1, tiled=True)[0]
    width = whole.shape[0]
    lower = jnp.linalg.cholesky(whole)
    inverse = jax.scipy.linalg.solve_triangular(
        lower, jnp.eye(width, dtype=jnp.float32), lower=True
    )
    ncol = lax.axis_size("col")
    nrow = lax.axis_size("row")
    col_index = lax.axis_index("col")
    tile_mask = jnp.repeat(jnp.repeat(pattern[0], BS, axis=0), BS, axis=1).astype(jnp.float32)
    masked = panel[0] * tile_mask
    rows_dev = masked.shape[0]
    full_rows = lax.all_gather(masked, "col", axis=1, tiled=True)
    factor_rows = lax.dot_general(full_rows, inverse, contract, precision=highest)
    share = width // ncol
    own_cols = lax.dynamic_slice_in_dim(factor_rows, col_index * share, share, 1)
    cw_dev = contribution.shape[2]
    head_piece = lax.dynamic_slice_in_dim(factor_rows, col_index * cw_dev, cw_dev, 0)
    head_rows = from_root(head_piece, "row", 0)
    update = contribution[0] - lax.dot_general(factor_rows, head_rows, contract, precision=highest)
    blk = rows_dev // BS
    cap = max(2, blk // nrow)
    pblk = blk // 2
    blocks = update.reshape(blk, BS * cw_dev)
    target = route[0, :, 0]
    place = slot[0]
    order_ids = jnp.arange(blk, dtype=jnp.int32)
    earlier = (target[None, :] == target[:, None]) & (order_ids[None, :] < order_ids[:, None])
    rank = jnp.sum(earlier.astype(jnp.int32), axis=1)
    half = target // nrow
    target_row = target % nrow
    position = target_row * (2 * cap) + half * cap + rank
    slots_all = jnp.arange(nrow * 2 * cap, dtype=jnp.int32)
    onehot = (position[None, :] == slots_all[:, None]).astype(jnp.float32)
    packed = jnp.dot(onehot, blocks, precision=highest).reshape(nrow, 2, cap, BS * cw_dev)
    labels = jnp.dot(onehot, (place + 1).astype(jnp.float32), precision=highest).reshape(
        nrow, 2, cap
    )
    mine = lax.axis_index("cube") % 2
    got, got_labels = (
        lax.all_to_all(packed, "row", split_axis=0, concat_axis=0, tiled=True),
        lax.all_to_all(labels, "row", split_axis=0, concat_axis=0, tiled=True),
    )
    keep = lax.dynamic_index_in_dim(got, mine, 1, keepdims=False)
    keep_labels = lax.dynamic_index_in_dim(got_labels, mine, 1, keepdims=False)
    other = lax.dynamic_index_in_dim(got, 1 - mine, 1, keepdims=False)
    other_labels = lax.dynamic_index_in_dim(got_labels, 1 - mine, 1, keepdims=False)
    back, back_labels = partner((other, other_labels), "cube", 0)
    incoming = jnp.concatenate([keep, back], axis=0).reshape(-1, BS * cw_dev)
    tags = jnp.concatenate([keep_labels, back_labels], axis=0).reshape(-1)
    wanted = jnp.arange(1, pblk + 1, dtype=jnp.float32)
    select = (tags[None, :] == wanted[:, None]).astype(jnp.float32)
    assembled = jnp.dot(select, incoming, precision=highest).reshape(pblk * BS, cw_dev)
    rows_here = diag_block.shape[1]
    diag_rows = lax.dynamic_slice_in_dim(
        lower, lax.axis_index(("row", "col")) * rows_here, rows_here, 0
    )
    return (diag_rows[None], own_cols[None], assembled[None])


def solution(mesh):
    small = mesh.shape["row"] == 2 and mesh.shape["col"] == 4
    return jax.shard_map(
        on_small if small else on_large,
        mesh=mesh,
        in_specs=(
            P("cube", ("row", "col"), None),
            P("cube", "row", "col"),
            P("cube", "row", "col"),
            P("cube", "row", "col"),
            P("cube", "row", None),
            P("cube", "row"),
        ),
        out_specs=(
            P("cube", ("row", "col"), None),
            P("cube", "row", "col"),
            P("cube", "row", "col"),
        ),
        check_vma=False,
    )
```
